256 devices in a mesh: alpha: 8 (over x_hi, y), beta: 32 (over z, x_lo, core).
Axes of the slice: x: 4 (x_hi: 2, x_lo: 2; x = x_hi * 2 + x_lo), y: 4, z: 8, core: 2. Of those that a mesh axis runs over, the one named last changes fastest.
Arguments:
- ci_vector: float32 [7168, 28672], P('alpha', 'beta'), may hold values from -6 to 6
- diagonal: float32 [7168, 28672], P('alpha', 'beta'), may hold values from -1.5 to 1.5
- energy: float32 [1], replicated, may hold values from -0.5 to 0.5
- alpha_partner: int32 [8, 2], P('alpha'), may hold values from 0 to 7, as said below
- alpha_coupling: bfloat16 [8, 2, 896, 896], P('alpha'), may hold values from -0.1875 to 0.1875
- alpha_mask: int32 [8, 2, 7, 7], P('alpha'), may hold values 0 or 1
- beta_partner: int32 [32, 2], P('beta'), may hold values from 0 to 31, as said below
- beta_coupling: bfloat16 [32, 2, 896, 896], P('beta', None, 'alpha'), may hold values from -0.1875 to 0.1875
- beta_mask: int32 [32, 2, 7, 7], P('beta'), may hold values 0 or 1
Outputs:
- correction: float32 [7168, 28672], P('alpha', 'beta')
The draws below stay inside these ranges and needn't reach their ends.
Inputs may be any that keep to these rules, and one draw needn't show every extreme that they name: alpha_partner[i, s] equals i with exactly one bit of its binary index flipped, and the two partners of a tile flip different bits. beta_partner[j, s] equals j with exactly one bit of its binary index flipped, and the two partners of a tile flip different bits.
All inputs are finite; a program needn't handle non-finite values. No bound on the sum of `alpha_mask` or of `beta_mask` on one device may be relied on, other than what follows from the above.
Results may differ from the reference program's by a relative error of at most 0.0003.
Values may be sent and summed in bfloat16 or wider, within the bound.
A program may use at most 128 MiB of HBM per device.

```python
import jax
import jax.numpy as jnp
from jax import lax

TILE = 896
BLOCK = 128
NBLK = 7
AT = 8
BT = 32
NA = 7168
NB = 28672


def partner_table(key, tile_count):
    bit_count = tile_count.bit_length() - 1
    top_bit = bit_count - 1
    key_group, key_offset, key_flip = jax.random.split(key, 3)
    indices = jnp.arange(tile_count, dtype=jnp.int32)
    group_bits = jax.random.randint(key_group, (2,), 0, top_bit, dtype=jnp.int32)
    upper = jnp.right_shift(indices, top_bit)
    bit_first = jnp.where(upper == 1, group_bits[1], group_bits[0])
    offsets = jax.random.randint(key_offset, (tile_count,), 1, bit_count, dtype=jnp.int32)
    bit_second = (bit_first + offsets) % bit_count
    first_partner = jnp.bitwise_xor(indices, jnp.left_shift(jnp.int32(1), bit_first))
    second_partner = jnp.bitwise_xor(indices, jnp.left_shift(jnp.int32(1), bit_second))
    flips = jax.random.randint(key_flip, (tile_count,), 0, 2, dtype=jnp.int32)
    slot_zero = jnp.where(flips == 1, second_partner, first_partner)
    slot_one = jnp.where(flips == 1, first_partner, second_partner)
    return jnp.stack([slot_zero, slot_one], axis=1).astype(jnp.int32)


def draw_alpha_partner(key, part):
    return partner_table(jax.random.fold_in(key, 11), AT)


def draw_beta_partner(key, part):
    return partner_table(jax.random.fold_in(key, 23), BT)


def plant(entries, stream_key, smallest, high):
    extent = entries.shape
    index_at = [jax.random.randint(jax.random.fold_in(stream_key, axis), (), 0, extent[axis]) for axis in range(len(extent))]
    entries = entries.at[tuple(index_at)].set(smallest)
    longest = extent.index(max(extent))
    index_at[longest] = (index_at[longest] + 1) % extent[longest]
    return entries.at[tuple(index_at)].set(high)


def block_levels(rng, dims, shards, least, largest):
    level = 1.0
    for axis_at, parts in shards:
        heights = jax.random.uniform(jax.random.fold_in(jax.random.fold_in(rng, 6), axis_at), (parts,), jnp.float32, least / len(shards), largest / len(shards))
        level = level * jnp.repeat(jnp.exp(heights), dims[axis_at] // parts).reshape((-1,) + (1,) * (len(dims) - 1 - axis_at))
    return level


def scatter_about(rng, dims, scale, bound, shards=(), held_as=jnp.bfloat16):
    loudness = block_levels(rng, dims, shards, -0.22, 0.18) if shards else 1.0
    array = jax.random.normal(rng, dims, jnp.float32) * scale * loudness
    return jnp.minimum(jnp.maximum(array, -bound), bound).astype(held_as)


def setup_inputs(seed: int = 0) -> dict:
    key_of = jax.random.split(jax.random.key(seed), 10)
    ci_vector = scatter_about(key_of[0], (NA, NB), 1.0, 6.0, ((0, 8), (1, 32)), jnp.float32)
    diagonal = jnp.clip(jax.random.uniform(key_of[1], (NA, NB), jnp.float32, -1.5, 1.5) * block_levels(key_of[1], (NA, NB), ((0, 8), (1, 32)), -0.4, 0.0), -1.5, 1.5)
    energy = jnp.clip(jax.random.uniform(key_of[2], (1,), jnp.float32, -0.5, 0.5), -0.5, 0.5)
    alpha_partner = draw_alpha_partner(jax.random.fold_in(key_of[9], 71), 0)
    alpha_coupling = scatter_about(key_of[4], (AT, 2, TILE, TILE), TILE ** -0.5, 0.1875, ((0, 8),))
    alpha_mask = plant((jax.random.randint(key_of[5], (AT, 2, NBLK, NBLK), 0, 4) < 3).astype(jnp.int32), jax.random.fold_in(key_of[5], 1), 0, 1)
    beta_partner = draw_beta_partner(jax.random.fold_in(key_of[9], 71), 0)
    beta_coupling = scatter_about(key_of[7], (BT, 2, TILE, TILE), TILE ** -0.5, 0.1875, ((0, 32), (2, 8)))
    beta_mask = plant((jax.random.randint(key_of[8], (BT, 2, NBLK, NBLK), 0, 4) < 3).astype(jnp.int32), jax.random.fold_in(key_of[8], 1), 0, 1)
    return dict(ci_vector=ci_vector, diagonal=diagonal, energy=energy, alpha_partner=alpha_partner, alpha_coupling=alpha_coupling, alpha_mask=alpha_mask, beta_partner=beta_partner, beta_coupling=beta_coupling, beta_mask=beta_mask)


def expand_mask(block_mask):
    values = block_mask.astype(jnp.float32)
    values = jnp.repeat(values, BLOCK, axis=-2)
    return jnp.repeat(values, BLOCK, axis=-1)


def reference(ci_vector, diagonal, energy, alpha_partner, alpha_coupling, alpha_mask, beta_partner, beta_coupling, beta_mask):
    highest = lax.Precision.HIGHEST

    def beta_column(column):
        summed = jnp.zeros((NA, TILE), jnp.float32)
        for slot_index in range(2):
            offset = (beta_partner[column, slot_index] * TILE).astype(jnp.int32)
            partner_cols = lax.dynamic_slice_in_dim(ci_vector, offset, TILE, 1)
            weights = beta_coupling[column, slot_index].astype(jnp.float32) * expand_mask(beta_mask[column, slot_index])
            summed = summed + jnp.dot(partner_cols, weights, precision=highest)
        return summed

    def alpha_row(row_tile):
        summed = jnp.zeros((TILE, NB), jnp.float32)
        for slot_index in range(2):
            offset = (alpha_partner[row_tile, slot_index] * TILE).astype(jnp.int32)
            partner_rows = lax.dynamic_slice_in_dim(ci_vector, offset, TILE, 0)
            weights = alpha_coupling[row_tile, slot_index].astype(jnp.float32) * expand_mask(alpha_mask[row_tile, slot_index])
            summed = summed + jnp.dot(weights.T, partner_rows, precision=highest)
        return summed

    beta_term = lax.map(beta_column, jnp.arange(BT, dtype=jnp.int32))
    beta_term = jnp.transpose(beta_term, (1, 0, 2)).reshape(NA, NB)
    alpha_term = lax.map(alpha_row, jnp.arange(AT, dtype=jnp.int32)).reshape(NA, NB)
    sigma = alpha_term + beta_term
    gap = diagonal - energy[0]
    return (sigma - energy[0] * ci_vector) * gap / (gap * gap + 0.0625)
```

```python
import jax
import jax.numpy as jnp
from jax import lax
from jax.experimental import pallas as pl
from jax.experimental.pallas import tpu as pltpu
from jax.sharding import PartitionSpec as P

MESH = pl.DeviceIdType.MESH
TILE = 896
BLOCK = 128
NBLK = TILE // BLOCK
HEAD = 16
CHUNKS = 7
ROWS = TILE // CHUNKS
PIECE = 112
LEVELS = 32767.0
F32 = jnp.float32
BF16 = jnp.bfloat16
K0, X1, X2, Y1, Y2, Z2, Z3, Z4 = range(8)
ZR = 8


def chunk_rows(c):
    return pl.ds(0, HEAD + ROWS) if c == 0 else pl.ds(HEAD + ROWS * c, ROWS)


def data_rows(c):
    return pl.ds(HEAD + ROWS * c, ROWS)


def flipped(index, bit):
    return index + (1 - 2 * ((index // bit) % 2)) * bit


def split(value):
    high = value.astype(BF16)
    return high, (value - high.astype(F32)).astype(BF16)


def pick(choices, rows):
    value = choices[0][1][rows, :]
    for chosen, ref in choices[1:]:
        value = lax.select(chosen, ref[rows, :], value)
    return value.astype(F32)


def decode(choices, rows):
    scale = jnp.exp2(pick(choices, pl.ds(0, HEAD)))[0:1, :]
    root = pick(choices, rows) * (1.0 / LEVELS)
    return (root * jnp.abs(root)) * (root * root) * scale


def kernel(
    ci_hbm, ac_hbm, bc_hbm, am, bm, ap, bp, out_hbm,
    cv, own, k0, x1, x2, y1, y2, z2, z3, z4, weights, piece, ha, hat, bl, xl, part, acc,
    load_sem, send_sem, recv_sem, wsend_sem, wrecv_sem, store_sem,
):
    tiles = [k0, x1, x2, y1, y2, z2, z3, z4]
    a = lax.axis_index("alpha")
    b = lax.axis_index("beta")
    y, xh = a % 4, a // 4
    core, xl_, z = b % 2, (b // 2) % 2, b // 4
    x = xh * 2 + xl_

    def at(dx=0, dy=0, dz=0, dc=0):
        nx, ny, nz = (x + dx + 4) % 4, (y + dy + 4) % 4, (z + dz + 8) % 8
        nc = (core + dc) % 2
        return ((nx // 2) * 4 + ny, nz * 4 + (nx % 2) * 2 + nc)

    tx = 1 - 2 * (x % 2)
    ty = 1 - 2 * (y % 2)
    tz = 1 - 2 * (z % 2)
    t = z % 4
    sz = 1 - 2 * (t // 2)
    inner = (t == 1) | (t == 2)

    load_c = pltpu.make_async_copy(ci_hbm, cv, load_sem.at[0])
    load_p = pltpu.make_async_copy(bc_hbm.at[0], piece, load_sem.at[1])
    load_a = pltpu.make_async_copy(ac_hbm.at[0], ha, load_sem.at[2])
    load_c.start()
    load_p.start()
    load_a.start()

    barrier = pltpu.get_barrier_semaphore()
    greet = [at(dc=1), at(dx=1), at(dx=-1), at(dx=2), at(dy=1), at(dy=-1), at(dz=1), at(dz=-1), at(dz=2), at(dz=-2)]
    for other in greet:
        pl.semaphore_signal(barrier, inc=1, device_id=other, device_id_type=MESH)

    def move(src, dst, lane, c, target):
        rows = chunk_rows(c)
        return pltpu.make_async_remote_copy(
            src_ref=src.at[rows, :],
            dst_ref=tiles[dst].at[rows, :],
            send_sem=send_sem.at[lane, c],
            recv_sem=recv_sem.at[dst, c],
            device_id=target,
            device_id_type=MESH,
        )

    def own_to_core(c):
        return move(own, K0, K0, c, at(dc=1))

    def own_to_x(c):
        return move(own, X1, X1, c, at(dx=tx))

    def pass_x(c):
        return move(x1, X2, X2, c, at(dx=-tx))

    def own_to_y(c):
        return move(own, Y1, Y1, c, at(dy=ty))

    def pass_y(c):
        return move(y1, Y2, Y2, c, at(dy=-ty))

    def own_to_z(c):
        return move(own, Z2, Z2, c, at(dz=tz))

    def own_to_z_far(c):
        return move(own, Z3, Z3, c, at(dz=2 * sz))

    def pass_z(c):
        return move(z2, Z3, ZR, c, at(dz=sz))

    def pass_z_far(c):
        return move(z3, Z4, Z4, c, at(dz=-2 * sz))

    def arrived(dst, c):
        rows = chunk_rows(c)
        pltpu.make_async_remote_copy(
            src_ref=tiles[dst].at[rows, :],
            dst_ref=tiles[dst].at[rows, :],
            send_sem=send_sem.at[dst, c],
            recv_sem=recv_sem.at[dst, c],
            device_id=at(dc=1),
            device_id_type=MESH,
        ).wait_recv()

    def wmove(ah, dy_src, lane, target):
        index = ((xh + ah) % 2) * 4 + (y + dy_src + 4) % 4
        rows = pl.ds(pl.multiple_of(index * PIECE, 16), PIECE)
        return pltpu.make_async_remote_copy(
            src_ref=weights.at[:, rows, :],
            dst_ref=weights.at[:, rows, :],
            send_sem=wsend_sem.at[lane],
            recv_sem=wrecv_sem.at[lane],
            device_id=target,
            device_id_type=MESH,
        )

    wsend = [
        wmove(0, 0, 0, at(dx=2)),
        wmove(0, 0, 1, at(dy=1)),
        wmove(0, 0, 2, at(dy=-1)),
        wmove(1, 0, 3, at(dy=1)),
        wmove(1, 0, 4, at(dy=-1)),
        wmove(0, -1, 5, at(dy=1)),
        wmove(1, 1, 6, at(dy=-1)),
    ]
    wrecv = [
        wmove(1, 0, 0, at(dx=2)),
        wmove(0, -1, 1, at(dy=1)),
        wmove(0, 1, 2, at(dy=1)),
        wmove(1, -1, 3, at(dy=1)),
        wmove(1, 1, 4, at(dy=1)),
        wmove(0, -2, 5, at(dy=1)),
        wmove(1, 2, 6, at(dy=1)),
    ]

    load_c.wait()

    def biggest(c, value):
        return jnp.maximum(value, jnp.max(jnp.abs(cv[pl.ds(pl.multiple_of(c * ROWS, ROWS), ROWS), :]), axis=0, keepdims=True))

    column = lax.fori_loop(0, CHUNKS, biggest, jnp.full((1, TILE), 1e-36, F32))
    top = jnp.max(column, axis=1, keepdims=True)
    exponent = jnp.maximum(jnp.floor(jnp.log2(top)) + 1.0, -120.0)
    exponent = jnp.broadcast_to(exponent, (HEAD, TILE))
    own[pl.ds(0, HEAD), :] = exponent.astype(jnp.int16)
    shrink = jnp.exp2(-exponent[0:1, :])

    def encode(c):
        value = cv[pl.ds(c * ROWS, ROWS), :]
        root = jnp.sqrt(jnp.sqrt(jnp.abs(value) * shrink)) * LEVELS
        root = jnp.minimum(jnp.round(root), LEVELS)
        own[data_rows(c), :] = jnp.where(value < 0, -root, root).astype(jnp.int16)

    def send_z(c):
        own_to_z(c).start()

        @pl.when(inner)
        def _():
            own_to_z_far(c).start()

    encode(0)
    pl.semaphore_wait(barrier, len(greet))
    send_z(0)
    encode(1)
    send_z(1)

    load_p.wait()
    for s in range(2):
        for k in range(PIECE // 16):
            row = a * PIECE + 16 * k
            u = row // BLOCK
            rows = pl.ds(pl.multiple_of(row, 16), 16)
            for v in range(NBLK):
                columns = pl.ds(v * BLOCK, BLOCK)
                block = piece[s, pl.ds(16 * k, 16), columns].astype(F32)
                weights[s, rows, columns] = (block * bm[0, s, u, v].astype(F32)).astype(BF16)
    for lane in (0, 1, 2):
        wsend[lane].start()
    for c in range(CHUNKS):
        if c >= 2:
            encode(c)
        own_to_x(c).start()
        own_to_y(c).start()
        own_to_core(c).start()

    load_a.wait()

    def mask_alpha(i, _):
        s, u = i // NBLK, i % NBLK
        rows = pl.ds(pl.multiple_of(u * BLOCK, BLOCK), BLOCK)
        to = pl.ds(pl.multiple_of(s * TILE + u * BLOCK, BLOCK), BLOCK)
        for v in range(NBLK):
            block = ha[s, rows, pl.ds(v * BLOCK, BLOCK)].astype(F32) * am[0, s, u, v].astype(F32)
            hat[pl.ds(v * BLOCK, BLOCK), to] = block.T.astype(BF16)
        return 0

    lax.fori_loop(0, 2 * NBLK, mask_alpha, 0)

    alpha_from = [[(ap[0, s] == flipped(a, bit), ref) for bit, ref in ((1, y1), (2, y2), (4, x2))] for s in range(2)]
    beta_from = [[(bp[0, s] == flipped(b, bit), ref) for bit, ref in ((1, k0), (2, x1), (4, z2), (8, z3), (16, z4))] for s in range(2)]

    def alpha_operand():
        def body(c, _):
            rows = pl.ds(pl.multiple_of(HEAD + c * ROWS, 16), ROWS)
            for s in range(2):
                high, low = split(decode(alpha_from[s], rows))
                to = pl.ds(pl.multiple_of(s * TILE + c * ROWS, ROWS), ROWS)
                for n in range(NBLK):
                    bl[n, to, pl.ds(0, BLOCK)] = high[:, n * BLOCK : (n + 1) * BLOCK]
                    bl[n, to, pl.ds(BLOCK, BLOCK)] = low[:, n * BLOCK : (n + 1) * BLOCK]
            return 0

        lax.fori_loop(0, CHUNKS, body, 0)

    def alpha_product(first, last):
        def body(i, _):
            n, m = i // 2, i % 2
            rows = pl.ds(pl.multiple_of(m * 448, 64), 448)
            both = jnp.dot(hat[rows, :], bl[n], preferred_element_type=F32)
            acc[rows, pl.ds(pl.multiple_of(n * BLOCK, BLOCK), BLOCK)] = both[:, :BLOCK] + both[:, BLOCK:]
            return 0

        lax.fori_loop(2 * first, 2 * last, body, 0)

    def beta_product(c):
        for s in range(2):
            high, low = split(decode(beta_from[s], data_rows(c)))
            xl[s, pl.ds(0, ROWS), :] = high
            xl[s, pl.ds(ROWS, ROWS), :] = low

        part[...] = jnp.zeros_like(part)
        for s in range(2):
            for k in (pl.ds(0, 512), pl.ds(512, TILE - 512)):
                part[...] += jnp.dot(xl[s, :, k], weights[s, k, :], preferred_element_type=F32)
        rows = pl.ds(c * ROWS, ROWS)
        acc[rows, :] = acc[rows, :] + (part[pl.ds(0, ROWS), :] + part[pl.ds(ROWS, ROWS), :])

    def store(c):
        rows = pl.ds(c * ROWS, ROWS)
        return pltpu.make_async_copy(acc.at[rows, :], out_hbm.at[rows, :], store_sem.at[c])

    for step in range(CHUNKS + 4):
        if 2 <= step + 1 < CHUNKS:
            send_z(step + 1)
        c = step - 1
        if 0 <= c < CHUNKS:

            @pl.when(inner)
            def _():
                arrived(Z2, c)
                pass_z(c).start()

        c = step - 2
        if 0 <= c < CHUNKS:
            arrived(Z3, c)
            pass_z_far(c).start()
        for c in (2 * step - 1, 2 * step):
            if 0 <= c < CHUNKS:
                arrived(X1, c)
                pass_x(c).start()
                arrived(Y1, c)
                pass_y(c).start()
        if step == 0:
            wrecv[0].wait_recv()
            wsend[3].start()
            wsend[4].start()
            wrecv[1].wait_recv()
            wsend[5].start()
        if step == 1:
            wrecv[4].wait_recv()
            wsend[6].start()
        if step == 4:
            for c in range(CHUNKS):
                arrived(X2, c)
                arrived(Y2, c)
            alpha_operand()
            alpha_product(0, 3)
            for lane in (2, 3, 5, 6):
                wrecv[lane].wait_recv()
        if step == 5:
            alpha_product(3, NBLK)
        for c in range(CHUNKS):
            if step == max(c + 4, 5):
                arrived(K0, c)

                @pl.when(jnp.logical_not(inner))
                def _():
                    arrived(Z2, c)

                arrived(Z4, c)
                beta_product(c)
                store(c).start()

    for c in range(CHUNKS):
        store(c).wait()
        for copy in (own_to_core(c), own_to_x(c), pass_x(c), own_to_y(c), pass_y(c), own_to_z(c), pass_z_far(c)):
            copy.wait_send()

        @pl.when(inner)
        def _():
            own_to_z_far(c).wait_send()
            pass_z(c).wait_send()

    for copy in wsend:
        copy.wait_send()


def local(ci_vector, diagonal, energy, alpha_partner, alpha_coupling, alpha_mask, beta_partner, beta_coupling, beta_mask):
    anywhere = pl.BlockSpec(memory_space=pl.ANY)
    scalars = pl.BlockSpec(memory_space=pltpu.SMEM)
    code = pltpu.VMEM((HEAD + TILE, TILE), jnp.int16)
    sigma = pl.pallas_call(
        kernel,
        out_shape=jax.ShapeDtypeStruct((TILE, TILE), F32),
        in_specs=[anywhere] * 3 + [scalars] * 4,
        out_specs=anywhere,
        scratch_shapes=[pltpu.VMEM((TILE, TILE), F32)]
        + [code] * 9
        + [
            pltpu.VMEM((2, TILE, TILE), BF16),
            pltpu.VMEM((2, PIECE, TILE), BF16),
            pltpu.VMEM((2, TILE, TILE), BF16),
            pltpu.VMEM((TILE, 2 * TILE), BF16),
            pltpu.VMEM((NBLK, 2 * TILE, 2 * BLOCK), BF16),
            pltpu.VMEM((2, 2 * ROWS, TILE), BF16),
            pltpu.VMEM((2 * ROWS, TILE), F32),
            pltpu.VMEM((TILE, TILE), F32),
            pltpu.SemaphoreType.DMA((3,)),
            pltpu.SemaphoreType.DMA((9, CHUNKS)),
            pltpu.SemaphoreType.DMA((8, CHUNKS)),
            pltpu.SemaphoreType.DMA((7,)),
            pltpu.SemaphoreType.DMA((7,)),
            pltpu.SemaphoreType.DMA((CHUNKS,)),
        ],
        compiler_params=pltpu.CompilerParams(collective_id=0, has_side_effects=True, vmem_limit_bytes=60 * 1024 * 1024),
    )(ci_vector, alpha_coupling, beta_coupling, alpha_mask, beta_mask, alpha_partner, beta_partner)
    gap = diagonal - energy[0]
    return (sigma - energy[0] * ci_vector) * gap / (gap * gap + 0.0625)


def solution(mesh):
    return jax.shard_map(
        local,
        mesh=mesh,
        in_specs=(
            P("alpha", "beta"),
            P("alpha", "beta"),
            P(),
            P("alpha", None),
            P("alpha", None, None, None),
            P("alpha", None, None, None),
            P("beta", None),
            P("beta", None, "alpha", None),
            P("beta", None, None, None),
        ),
        out_specs=P("alpha", "beta"),
        check_vma=False,
    )
```

```python
import jax
import jax.numpy as jnp
from jax import lax
from jax.experimental import pallas as pl
from jax.experimental.pallas import tpu as pltpu
from jax.sharding import PartitionSpec as P

MESH = pl.DeviceIdType.MESH
TILE = 896
BLOCK = 128
NBLK = TILE // BLOCK
HEAD = 16
CHUNKS = 14
ROWS = TILE // CHUNKS
PARTS = 7
PROWS = TILE // PARTS
PIECE = 112
LEVELS = 32767.0
F32 = jnp.float32
BF16 = jnp.bfloat16
K0, X1, X2, Y1, Y2, Z2, Z3, Z4 = range(8)
ZR = 8


def chunk_rows(c):
    return pl.ds(0, HEAD + ROWS) if c == 0 else pl.ds(HEAD + ROWS * c, ROWS)


def data_rows(c):
    return pl.ds(HEAD + ROWS * c, ROWS)


def flipped(index, bit):
    return index + (1 - 2 * ((index // bit) % 2)) * bit


def split(value):
    high = value.astype(BF16)
    return high, (value - high.astype(F32)).astype(BF16)


def pick(choices, rows):
    value = choices[0][1][rows, :]
    for chosen, ref in choices[1:]:
        value = lax.select(chosen, ref[rows, :], value)
    return value.astype(F32)


def decode(choices, rows):
    scale = jnp.exp2(pick(choices, pl.ds(0, HEAD)))[0:1, :]
    root = pick(choices, rows) * (1.0 / LEVELS)
    return (root * jnp.abs(root)) * (root * root) * scale


def kernel(
    ci_hbm, diag_hbm, ac_hbm, bc_hbm, am, bm, ap, bp, energy, out_hbm,
    cv, dv, own, k0, x1, x2, y1, y2, z2, z3, z4, weights, piece, ha, hat, bl, xl, part, acc,
    load_sem, send_sem, recv_sem, wsend_sem, wrecv_sem, store_sem,
):
    tiles = [k0, x1, x2, y1, y2, z2, z3, z4]
    a = lax.axis_index("alpha")
    b = lax.axis_index("beta")
    y, xh = a % 4, a // 4
    core, xl_, z = b % 2, (b // 2) % 2, b // 4
    x = xh * 2 + xl_

    def at(dx=0, dy=0, dz=0, dc=0):
        nx, ny, nz = (x + dx + 4) % 4, (y + dy + 4) % 4, (z + dz + 8) % 8
        nc = (core + dc) % 2
        return ((nx // 2) * 4 + ny, nz * 4 + (nx % 2) * 2 + nc)

    tx = 1 - 2 * (x % 2)
    ty = 1 - 2 * (y % 2)
    tz = 1 - 2 * (z % 2)
    t = z % 4
    sz = 1 - 2 * (t // 2)
    inner = (t == 1) | (t == 2)

    load_c = pltpu.make_async_copy(ci_hbm, cv, load_sem.at[0])
    load_p = pltpu.make_async_copy(bc_hbm.at[0], piece, load_sem.at[1])
    load_a = pltpu.make_async_copy(ac_hbm.at[0], ha, load_sem.at[2])
    load_d = pltpu.make_async_copy(diag_hbm, dv, load_sem.at[3])
    load_c.start()
    load_p.start()
    load_a.start()
    load_d.start()

    barrier = pltpu.get_barrier_semaphore()
    greet = [at(dc=1), at(dx=1), at(dx=-1), at(dx=2), at(dy=1), at(dy=-1), at(dz=1), at(dz=-1), at(dz=2), at(dz=-2)]
    for other in greet:
        pl.semaphore_signal(barrier, inc=1, device_id=other, device_id_type=MESH)

    def move(src, dst, lane, c, target):
        rows = chunk_rows(c)
        return pltpu.make_async_remote_copy(
            src_ref=src.at[rows, :],
            dst_ref=tiles[dst].at[rows, :],
            send_sem=send_sem.at[lane, c],
            recv_sem=recv_sem.at[dst, c],
            device_id=target,
            device_id_type=MESH,
        )

    def own_to_core(c):
        return move(own, K0, K0, c, at(dc=1))

    def own_to_x(c):
        return move(own, X1, X1, c, at(dx=tx))

    def pass_x(c):
        return move(x1, X2, X2, c, at(dx=-tx))

    def own_to_y(c):
        return move(own, Y1, Y1, c, at(dy=ty))

    def pass_y(c):
        return move(y1, Y2, Y2, c, at(dy=-ty))

    def own_to_z(c):
        return move(own, Z2, Z2, c, at(dz=tz))

    def own_to_z_far(c):
        return move(own, Z3, Z3, c, at(dz=2 * sz))

    def pass_z(c):
        return move(z2, Z3, ZR, c, at(dz=sz))

    def pass_z_far(c):
        return move(z3, Z4, Z4, c, at(dz=-2 * sz))

    def arrived(dst, c):
        rows = chunk_rows(c)
        pltpu.make_async_remote_copy(
            src_ref=tiles[dst].at[rows, :],
            dst_ref=tiles[dst].at[rows, :],
            send_sem=send_sem.at[dst, c],
            recv_sem=recv_sem.at[dst, c],
            device_id=at(dc=1),
            device_id_type=MESH,
        ).wait_recv()

    def wmove(ah, dy_src, lane, target):
        index = ((xh + ah) % 2) * 4 + (y + dy_src + 4) % 4
        rows = pl.ds(pl.multiple_of(index * PIECE, 16), PIECE)
        return pltpu.make_async_remote_copy(
            src_ref=weights.at[:, rows, :],
            dst_ref=weights.at[:, rows, :],
            send_sem=wsend_sem.at[lane],
            recv_sem=wrecv_sem.at[lane],
            device_id=target,
            device_id_type=MESH,
        )

    wsend = [
        wmove(0, 0, 0, at(dx=2)),
        wmove(0, 0, 1, at(dy=1)),
        wmove(0, 0, 2, at(dy=-1)),
        wmove(1, 0, 3, at(dy=1)),
        wmove(1, 0, 4, at(dy=-1)),
        wmove(0, -1, 5, at(dy=1)),
        wmove(1, 1, 6, at(dy=-1)),
    ]
    wrecv = [
        wmove(1, 0, 0, at(dx=2)),
        wmove(0, -1, 1, at(dy=1)),
        wmove(0, 1, 2, at(dy=1)),
        wmove(1, -1, 3, at(dy=1)),
        wmove(1, 1, 4, at(dy=1)),
        wmove(0, -2, 5, at(dy=1)),
        wmove(1, 2, 6, at(dy=1)),
    ]

    load_c.wait()

    def biggest(c, value):
        return jnp.maximum(value, jnp.max(jnp.abs(cv[pl.ds(pl.multiple_of(c * PROWS, PROWS), PROWS), :]), axis=0, keepdims=True))

    column = lax.fori_loop(0, PARTS, biggest, jnp.full((1, TILE), 1e-36, F32))
    top = jnp.max(column, axis=1, keepdims=True)
    exponent = jnp.maximum(jnp.floor(jnp.log2(top)) + 1.0, -120.0)
    exponent = jnp.broadcast_to(exponent, (HEAD, TILE))
    own[pl.ds(0, HEAD), :] = exponent.astype(jnp.int16)
    shrink = jnp.exp2(-exponent[0:1, :])

    def encode(c):
        value = cv[pl.ds(c * ROWS, ROWS), :]
        root = jnp.sqrt(jnp.sqrt(jnp.abs(value) * shrink)) * LEVELS
        root = jnp.minimum(jnp.round(root), LEVELS)
        own[data_rows(c), :] = jnp.where(value < 0, -root, root).astype(jnp.int16)

    def send_z(c):
        @pl.when(inner)
        def _():
            own_to_z_far(c).start()

        @pl.when(jnp.logical_not(inner))
        def _():
            own_to_z(c).start()

    encode(0)
    pl.semaphore_wait(barrier, len(greet))
    send_z(0)
    for c in range(1, CHUNKS):
        encode(c)
        send_z(c)

    load_p.wait()
    for s in range(2):
        for k in range(PIECE // 16):
            row = a * PIECE + 16 * k
            u = row // BLOCK
            rows = pl.ds(pl.multiple_of(row, 16), 16)
            for v in range(NBLK):
                columns = pl.ds(v * BLOCK, BLOCK)
                block = piece[s, pl.ds(16 * k, 16), columns].astype(F32)
                weights[s, rows, columns] = (block * bm[0, s, u, v].astype(F32)).astype(BF16)
    for lane in (0, 1, 2):
        wsend[lane].start()
    for c in range(CHUNKS):
        own_to_x(c).start()
        own_to_y(c).start()
        own_to_core(c).start()

    load_a.wait()

    def mask_alpha(i):
        s, u = i // NBLK, i % NBLK
        for v in range(NBLK):
            block = ha[s, pl.ds(u * BLOCK, BLOCK), pl.ds(v * BLOCK, BLOCK)].astype(F32) * am[0, s, u, v].astype(F32)
            hat[pl.ds(v * BLOCK, BLOCK), pl.ds(s * TILE + u * BLOCK, BLOCK)] = block.T.astype(BF16)

    alpha_from = [[(ap[0, s] == flipped(a, bit), ref) for bit, ref in ((1, y1), (2, y2), (4, x2))] for s in range(2)]
    beta_from = [[(bp[0, s] == flipped(b, bit), ref) for bit, ref in ((1, k0), (2, x1), (4, z2), (8, z3), (16, z4))] for s in range(2)]

    def alpha_operand():
        def body(c, _):
            rows = pl.ds(pl.multiple_of(HEAD + c * PROWS, 16), PROWS)
            for s in range(2):
                high, low = split(decode(alpha_from[s], rows))
                to = pl.ds(pl.multiple_of(s * TILE + c * PROWS, PROWS), PROWS)
                for n in range(NBLK):
                    bl[n, to, pl.ds(0, BLOCK)] = high[:, n * BLOCK : (n + 1) * BLOCK]
                    bl[n, to, pl.ds(BLOCK, BLOCK)] = low[:, n * BLOCK : (n + 1) * BLOCK]
            return 0

        lax.fori_loop(0, PARTS, body, 0)

    def alpha_product(first, last):
        def body(i, _):
            n, m = i // 2, i % 2
            rows = pl.ds(pl.multiple_of(m * 448, 64), 448)
            both = jnp.dot(hat[rows, :], bl[n], preferred_element_type=F32)
            acc[rows, pl.ds(pl.multiple_of(n * BLOCK, BLOCK), BLOCK)] = both[:, :BLOCK] + both[:, BLOCK:]
            return 0

        lax.fori_loop(2 * first, 2 * last, body, 0)

    def beta_product(p):
        for s in range(2):
            high, low = split(decode(beta_from[s], pl.ds(HEAD + p * PROWS, PROWS)))
            xl[s, pl.ds(0, PROWS), :] = high
            xl[s, pl.ds(PROWS, PROWS), :] = low

        part[...] = jnp.zeros_like(part)
        for s in range(2):
            for k in (pl.ds(0, 512), pl.ds(512, TILE - 512)):
                part[...] += jnp.dot(xl[s, :, k], weights[s, k, :], preferred_element_type=F32)
        rows = pl.ds(p * PROWS, PROWS)
        sigma = acc[rows, :] + (part[pl.ds(0, PROWS), :] + part[pl.ds(PROWS, PROWS), :])
        gap = dv[rows, :] - energy[0]
        acc[rows, :] = (sigma - energy[0] * cv[rows, :]) * gap / (gap * gap + 0.0625)

    def store(p):
        rows = pl.ds(p * PROWS, PROWS)
        return pltpu.make_async_copy(acc.at[rows, :], out_hbm.at[rows, :], store_sem.at[p])

    far, side = 2, 4
    for step in range(CHUNKS + side):
        c = step
        if c < CHUNKS:

            @pl.when(inner)
            def _():
                arrived(Z2, c)
                pass_z(c).start()

        c = step - far
        if 0 <= c < CHUNKS:
            arrived(Z3, c)
            pass_z_far(c).start()

            @pl.when(inner)
            def _():
                own_to_z(c).start()

        c = step - side
        if 0 <= c < CHUNKS:
            arrived(X1, c)
            pass_x(c).start()
            arrived(Y1, c)
            pass_y(c).start()
        if step < 2 * NBLK:
            mask_alpha(step)
        if step == 2:
            wrecv[0].wait_recv()
            wsend[3].start()
            wsend[4].start()
        if step == 4:
            wrecv[1].wait_recv()
            wsend[5].start()
        if step == 6:
            wrecv[4].wait_recv()
            wsend[6].start()

    for c in range(CHUNKS):
        arrived(X2, c)
        arrived(Y2, c)
    alpha_operand()
    alpha_product(0, NBLK)
    for lane in (2, 3, 5, 6):
        wrecv[lane].wait_recv()
    load_d.wait()
    for p in range(PARTS):
        for c in (2 * p, 2 * p + 1):
            arrived(K0, c)

            @pl.when(jnp.logical_not(inner))
            def _():
                arrived(Z2, c)

            arrived(Z4, c)
        beta_product(p)
        store(p).start()

    for p in range(PARTS):
        store(p).wait()
    for c in range(CHUNKS):
        for copy in (own_to_core(c), own_to_x(c), pass_x(c), own_to_y(c), pass_y(c), own_to_z(c), pass_z_far(c)):
            copy.wait_send()

        @pl.when(inner)
        def _():
            own_to_z_far(c).wait_send()
            pass_z(c).wait_send()

    for copy in wsend:
        copy.wait_send()


def local(ci_vector, diagonal, energy, alpha_partner, alpha_coupling, alpha_mask, beta_partner, beta_coupling, beta_mask):
    anywhere = pl.BlockSpec(memory_space=pl.ANY)
    scalars = pl.BlockSpec(memory_space=pltpu.SMEM)
    code = pltpu.VMEM((HEAD + TILE, TILE), jnp.int16)
    return pl.pallas_call(
        kernel,
        out_shape=jax.ShapeDtypeStruct((TILE, TILE), F32),
        in_specs=[anywhere] * 4 + [scalars] * 5,
        out_specs=anywhere,
        scratch_shapes=[pltpu.VMEM((TILE, TILE), F32)] * 2
        + [code] * 9
        + [
            pltpu.VMEM((2, TILE, TILE), BF16),
            pltpu.VMEM((2, PIECE, TILE), BF16),
            pltpu.VMEM((2, TILE, TILE), BF16),
            pltpu.VMEM((TILE, 2 * TILE), BF16),
            pltpu.VMEM((NBLK, 2 * TILE, 2 * BLOCK), BF16),
            pltpu.VMEM((2, 2 * PROWS, TILE), BF16),
            pltpu.VMEM((2 * PROWS, TILE), F32),
            pltpu.VMEM((TILE, TILE), F32),
            pltpu.SemaphoreType.DMA((4,)),
            pltpu.SemaphoreType.DMA((9, CHUNKS)),
            pltpu.SemaphoreType.DMA((8, CHUNKS)),
            pltpu.SemaphoreType.DMA((7,)),
            pltpu.SemaphoreType.DMA((7,)),
            pltpu.SemaphoreType.DMA((PARTS,)),
        ],
        compiler_params=pltpu.CompilerParams(collective_id=0, has_side_effects=True, vmem_limit_bytes=60 * 1024 * 1024),
    )(ci_vector, diagonal, alpha_coupling, beta_coupling, alpha_mask, beta_mask, alpha_partner, beta_partner, energy)


def solution(mesh):
    return jax.shard_map(
        local,
        mesh=mesh,
        in_specs=(
            P("alpha", "beta"),
            P("alpha", "beta"),
            P(),
            P("alpha", None),
            P("alpha", None, None, None),
            P("alpha", None, None, None),
            P("beta", None),
            P("beta", None, "alpha", None),
            P("beta", None, None, None),
        ),
        out_specs=P("alpha", "beta"),
        check_vma=False,
    )
```

```python
import jax
import jax.numpy as jnp
from jax import lax
from jax.experimental import pallas as pl
from jax.experimental.pallas import tpu as pltpu
from jax.sharding import PartitionSpec as P

MESH = pl.DeviceIdType.MESH
TILE = 896
BLOCK = 128
NBLK = TILE // BLOCK
CHUNKS = 14
ROWS = TILE // CHUNKS
PARTS = 7
PROWS = TILE // PARTS
START, EARLY = 9, 4
PIECE = 112
LEVELS = 32767.0
F32 = jnp.float32
BF16 = jnp.bfloat16
K0, X1, X2, Y1, Y2, Z2, Z3, Z4 = range(8)
ZR = 8


def chunk_rows(c):
    return pl.ds(ROWS * c, ROWS)


def flipped(index, bit):
    return index + (1 - 2 * ((index // bit) % 2)) * bit


def split(value):
    high = value.astype(BF16)
    return high, (value - high.astype(F32)).astype(BF16)


def pick(choices, rows, at):
    value = choices[0][at][rows, :]
    for choice in choices[1:]:
        value = lax.select(choice[0], choice[at][rows, :], value)
    return value.astype(F32)


def decode(choices, rows):
    scale = pick(choices, pl.ds(0, 8), 2)[0:1, 0:1]
    root = pick(choices, rows, 1) * (1.0 / LEVELS)
    return (root * jnp.abs(root)) * (root * root) * scale


def kernel(
    ci_hbm, diag_hbm, ac_hbm, bc_hbm, am, bm, ap, bp, energy, out_hbm,
    cv, dv, own, k0, x1, x2, y1, y2, z2, z3, z4, weights, piece, ha, hat, bl, xl, part, acc,
    head, h0, h1, h2, h3, h4, h5, h6, h7, load_sem, part_sem, send_sem, recv_sem, wsend_sem, wrecv_sem, hsend_sem, hrecv_sem, store_sem,
):
    tiles = [k0, x1, x2, y1, y2, z2, z3, z4]
    heads = [h0, h1, h2, h3, h4, h5, h6, h7]
    a = lax.axis_index("alpha")
    b = lax.axis_index("beta")
    y, xh = a % 4, a // 4
    core, xl_, z = b % 2, (b // 2) % 2, b // 4
    x = xh * 2 + xl_

    def at(dx=0, dy=0, dz=0, dc=0):
        nx, ny, nz = (x + dx + 4) % 4, (y + dy + 4) % 4, (z + dz + 8) % 8
        nc = (core + dc) % 2
        return ((nx // 2) * 4 + ny, nz * 4 + (nx % 2) * 2 + nc)

    tx = 1 - 2 * (x % 2)
    ty = 1 - 2 * (y % 2)
    tz = 1 - 2 * (z % 2)
    t = z % 4
    sz = 1 - 2 * (t // 2)
    inner = (t == 1) | (t == 2)

    def load_c(c):
        rows = pl.ds(c * PROWS, PROWS)
        return pltpu.make_async_copy(ci_hbm.at[rows, :], cv.at[rows, :], part_sem.at[c])

    load_p = pltpu.make_async_copy(bc_hbm.at[0], piece, load_sem.at[1])
    load_a = pltpu.make_async_copy(ac_hbm.at[0], ha, load_sem.at[2])
    load_d = pltpu.make_async_copy(diag_hbm, dv, load_sem.at[3])
    for c in range(PARTS):
        load_c(c).start()
    load_p.start()
    load_a.start()
    load_d.start()

    barrier = pltpu.get_barrier_semaphore()
    greet = [at(dc=1), at(dx=1), at(dx=-1), at(dx=2), at(dy=1), at(dy=-1), at(dy=2), at(dz=1), at(dz=-1), at(dz=2), at(dz=-2), at(dz=4)]
    for other in greet:
        pl.semaphore_signal(barrier, inc=1, device_id=other, device_id_type=MESH)

    def move(src, dst, lane, c, target):
        rows = chunk_rows(c)
        return pltpu.make_async_remote_copy(
            src_ref=src.at[rows, :],
            dst_ref=tiles[dst].at[rows, :],
            send_sem=send_sem.at[lane, c],
            recv_sem=recv_sem.at[dst, c],
            device_id=target,
            device_id_type=MESH,
        )

    def own_to_core(c):
        return move(own, K0, K0, c, at(dc=1))

    def own_to_x(c):
        return move(own, X1, X1, c, at(dx=tx))

    def pass_x(c):
        return move(x1, X2, X2, c, at(dx=-tx))

    def own_to_y(c):
        return move(own, Y1, Y1, c, at(dy=ty))

    def pass_y(c):
        return move(y1, Y2, Y2, c, at(dy=-ty))

    def own_to_z(c):
        return move(own, Z2, Z2, c, at(dz=tz))

    def own_to_z_far(c):
        return move(own, Z3, Z3, c, at(dz=2 * sz))

    def pass_z(c):
        return move(z2, Z3, ZR, c, at(dz=sz))

    def pass_z_far(c):
        return move(z3, Z4, Z4, c, at(dz=-2 * sz))

    def arrived(dst, c):
        rows = chunk_rows(c)
        pltpu.make_async_remote_copy(
            src_ref=tiles[dst].at[rows, :],
            dst_ref=tiles[dst].at[rows, :],
            send_sem=send_sem.at[dst, c],
            recv_sem=recv_sem.at[dst, c],
            device_id=at(dc=1),
            device_id_type=MESH,
        ).wait_recv()

    def wmove(ah, dy_src, lane, target):
        index = ((xh + ah) % 2) * 4 + (y + dy_src + 4) % 4
        rows = pl.ds(pl.multiple_of(index * PIECE, 16), PIECE)
        return pltpu.make_async_remote_copy(
            src_ref=weights.at[:, rows, :],
            dst_ref=weights.at[:, rows, :],
            send_sem=wsend_sem.at[lane],
            recv_sem=wrecv_sem.at[lane],
            device_id=target,
            device_id_type=MESH,
        )

    wsend = [
        wmove(0, 0, 0, at(dx=2)),
        wmove(0, 0, 1, at(dy=1)),
        wmove(0, 0, 2, at(dy=-1)),
        wmove(1, 0, 3, at(dy=1)),
        wmove(1, 0, 4, at(dy=-1)),
        wmove(0, -1, 5, at(dy=1)),
        wmove(1, 1, 6, at(dy=-1)),
    ]
    wrecv = [
        wmove(1, 0, 0, at(dx=2)),
        wmove(0, -1, 1, at(dy=1)),
        wmove(0, 1, 2, at(dy=1)),
        wmove(1, -1, 3, at(dy=1)),
        wmove(1, 1, 4, at(dy=1)),
        wmove(0, -2, 5, at(dy=1)),
        wmove(1, 2, 6, at(dy=1)),
    ]

    hsend = [
        pltpu.make_async_remote_copy(
            src_ref=head,
            dst_ref=heads[dst],
            send_sem=hsend_sem.at[dst],
            recv_sem=hrecv_sem.at[dst],
            device_id=target,
            device_id_type=MESH,
        )
        for dst, target in (
            (K0, at(dc=1)),
            (X1, at(dx=tx)),
            (X2, at(dx=2)),
            (Y1, at(dy=ty)),
            (Y2, at(dy=2)),
            (Z2, at(dz=tz)),
            (Z3, at(dz=2 - 4 * ((z // 2) % 2))),
            (Z4, at(dz=4)),
        )
    ]
    column = jnp.full((1, TILE), 1e-36, F32)
    for c in range(PARTS):
        load_c(c).wait()
        column = jnp.maximum(column, jnp.max(jnp.abs(cv[pl.ds(c * PROWS, PROWS), :]), axis=0, keepdims=True))
    top = jnp.max(column, axis=1, keepdims=True)
    exponent = jnp.maximum(jnp.floor(jnp.log2(top)) + 1.0, -120.0)
    head[...] = jnp.broadcast_to(jnp.exp2(exponent), (8, BLOCK))
    shrink = jnp.exp2(-exponent)

    def encode(c):
        value = cv[pl.ds(c * ROWS, ROWS), :]
        root = jnp.sqrt(jnp.sqrt(jnp.abs(value) * shrink)) * LEVELS
        root = jnp.minimum(jnp.round(root), LEVELS)
        own[chunk_rows(c), :] = jnp.where(value < 0, -root, root).astype(jnp.int16)

    def send_z(c):
        @pl.when(inner)
        def _():
            own_to_z_far(c).start()

        @pl.when(jnp.logical_not(inner))
        def _():
            own_to_z(c).start()

    encode(0)
    pl.semaphore_wait(barrier, len(greet))
    send_z(0)
    for c in range(1, CHUNKS):
        encode(c)
        send_z(c)

    load_p.wait()
    for s in range(2):
        for k in range(PIECE // 16):
            row = a * PIECE + 16 * k
            u = row // BLOCK
            rows = pl.ds(pl.multiple_of(row, 16), 16)
            for v in range(NBLK):
                columns = pl.ds(v * BLOCK, BLOCK)
                block = piece[s, pl.ds(16 * k, 16), columns].astype(F32)
                weights[s, rows, columns] = (block * bm[0, u, s, v].astype(F32)).astype(BF16)
    for lane in (0, 1, 2):
        wsend[lane].start()
    for copy in hsend:
        copy.start()
    for c in range(CHUNKS):
        own_to_x(c).start()
        own_to_y(c).start()
        own_to_core(c).start()

    load_a.wait()

    def mask_alpha(i):
        s, u = i // NBLK, i % NBLK
        for v in range(NBLK):
            block = ha[s, pl.ds(u * BLOCK, BLOCK), pl.ds(v * BLOCK, BLOCK)].astype(F32) * am[0, u, s, v].astype(F32)
            hat[pl.ds(v * BLOCK, BLOCK), pl.ds(s * TILE + u * BLOCK, BLOCK)] = block.T.astype(BF16)

    alpha_from = [[(ap[0, s] == flipped(a, bit), tiles[t], heads[t]) for bit, t in ((1, Y1), (2, Y2), (4, X2))] for s in range(2)]
    beta_from = [[(bp[0, s] == flipped(b, bit), tiles[t], heads[t]) for bit, t in ((1, K0), (2, X1), (4, Z2), (8, Z3), (16, Z4))] for s in range(2)]

    def alpha_operand():
        def body(c, _):
            rows = pl.ds(pl.multiple_of(c * PROWS, PROWS), PROWS)
            for s in range(2):
                high, low = split(decode(alpha_from[s], rows))
                to = pl.ds(pl.multiple_of(s * TILE + c * PROWS, PROWS), PROWS)
                for n in range(NBLK):
                    bl[n, to, pl.ds(0, BLOCK)] = high[:, n * BLOCK : (n + 1) * BLOCK]
                    bl[n, to, pl.ds(BLOCK, BLOCK)] = low[:, n * BLOCK : (n + 1) * BLOCK]
            return 0

        lax.fori_loop(0, PARTS, body, 0)

    def alpha_product(first, last):
        def body(i, _):
            n, m = i // 2, i % 2
            rows = pl.ds(pl.multiple_of(m * 448, 64), 448)
            both = jnp.dot(hat[rows, :], bl[n], preferred_element_type=F32)
            acc[rows, pl.ds(pl.multiple_of(n * BLOCK, BLOCK), BLOCK)] += both[:, :BLOCK] + both[:, BLOCK:]
            return 0

        lax.fori_loop(2 * first, 2 * last, body, 0)

    def beta_product(first, count):
        rows = pl.ds(first, count)
        for s in range(2):
            high, low = split(decode(beta_from[s], rows))
            xl[s, pl.ds(0, count), :] = high
            xl[s, pl.ds(count, count), :] = low

        both = pl.ds(0, 2 * count)
        for s in range(2):
            for k in (pl.ds(0, 512), pl.ds(512, TILE - 512)):
                product = jnp.dot(xl[s, both, k], weights[s, k, :], preferred_element_type=F32)
                if s == 0 and k.start == 0:
                    part[both, :] = product
                else:
                    part[both, :] += product
        acc[rows, :] += part[pl.ds(0, count), :] + part[pl.ds(count, count), :]

    def correct(first, count):
        rows = pl.ds(first, count)
        gap = dv[rows, :] - energy[0]
        acc[rows, :] = (acc[rows, :] - energy[0] * cv[rows, :]) * gap / (gap * gap + 0.0625)

    def complete(c):
        arrived(K0, c)

        @pl.when(jnp.logical_not(inner))
        def _():
            arrived(Z2, c)

        arrived(Z4, c)

    def store(c):
        rows = chunk_rows(c)
        return pltpu.make_async_copy(acc.at[rows, :], out_hbm.at[rows, :], store_sem.at[c])

    acc[...] = jnp.zeros_like(acc)
    far, side = 2, 4
    for step in range(CHUNKS + side):
        c = step
        if c < CHUNKS:

            @pl.when(inner)
            def _():
                arrived(Z2, c)
                pass_z(c).start()

        c = step - far
        if 0 <= c < CHUNKS:
            arrived(Z3, c)
            pass_z_far(c).start()

            @pl.when(inner)
            def _():
                own_to_z(c).start()

        c = step - side
        if 0 <= c < CHUNKS:
            arrived(X1, c)
            pass_x(c).start()
            arrived(Y1, c)
            pass_y(c).start()
        if step < 2 * NBLK:
            mask_alpha(step)
        if step == 2:
            wrecv[0].wait_recv()
            wsend[3].start()
            wsend[4].start()
        if step == 4:
            wrecv[1].wait_recv()
            wsend[5].start()
        if step == 6:
            wrecv[4].wait_recv()
            wsend[6].start()
        if step == START:
            for dst in range(8):
                hsend[dst].wait_recv()
            for lane in (2, 3, 5, 6):
                wrecv[lane].wait_recv()
        if step >= START and (step - START) % 2 == 0 and (step - START) // 2 < EARLY:
            p = (step - START) // 2
            complete(2 * p)
            complete(2 * p + 1)
            beta_product(p * PROWS, PROWS)

    for c in range(CHUNKS):
        arrived(X2, c)
        arrived(Y2, c)
    alpha_operand()
    alpha_product(0, NBLK)
    load_d.wait()
    for p in range(EARLY):
        correct(p * PROWS, PROWS)
        for c in (2 * p, 2 * p + 1):
            store(c).start()
    for group in [(c, c + 1) for c in range(2 * EARLY, CHUNKS - 2, 2)] + [(CHUNKS - 2,), (CHUNKS - 1,)]:
        for c in group:
            complete(c)
        beta_product(group[0] * ROWS, len(group) * ROWS)
        correct(group[0] * ROWS, len(group) * ROWS)
        for c in group:
            store(c).start()

    for copy in hsend:
        copy.wait_send()
    for c in range(CHUNKS):
        store(c).wait()
    for c in range(CHUNKS):
        for copy in (own_to_core(c), own_to_x(c), pass_x(c), own_to_y(c), pass_y(c), own_to_z(c), pass_z_far(c)):
            copy.wait_send()

        @pl.when(inner)
        def _():
            own_to_z_far(c).wait_send()
            pass_z(c).wait_send()

    for copy in wsend:
        copy.wait_send()


def local(ci_vector, diagonal, energy, alpha_partner, alpha_coupling, alpha_mask, beta_partner, beta_coupling, beta_mask):
    anywhere = pl.BlockSpec(memory_space=pltpu.HBM)
    scalars = pl.BlockSpec(memory_space=pltpu.SMEM)
    code = pltpu.VMEM((TILE, TILE), jnp.int16)
    return pl.pallas_call(
        kernel,
        out_shape=jax.ShapeDtypeStruct((TILE, TILE), F32),
        in_specs=[anywhere] * 4 + [scalars] * 5,
        out_specs=anywhere,
        scratch_shapes=[pltpu.VMEM((TILE, TILE), F32)] * 2
        + [code] * 9
        + [
            pltpu.VMEM((2, TILE, TILE), BF16),
            pltpu.VMEM((2, PIECE, TILE), BF16),
            pltpu.VMEM((2, TILE, TILE), BF16),
            pltpu.VMEM((TILE, 2 * TILE), BF16),
            pltpu.VMEM((NBLK, 2 * TILE, 2 * BLOCK), BF16),
            pltpu.VMEM((2, 2 * PROWS, TILE), BF16),
            pltpu.VMEM((2 * PROWS, TILE), F32),
            pltpu.VMEM((TILE, TILE), F32),
        ]
        + [pltpu.VMEM((8, BLOCK), F32)] * 9
        + [
            pltpu.SemaphoreType.DMA((4,)),
            pltpu.SemaphoreType.DMA((PARTS,)),
            pltpu.SemaphoreType.DMA((9, CHUNKS)),
            pltpu.SemaphoreType.DMA((8, CHUNKS)),
            pltpu.SemaphoreType.DMA((7,)),
            pltpu.SemaphoreType.DMA((7,)),
            pltpu.SemaphoreType.DMA((8,)),
            pltpu.SemaphoreType.DMA((8,)),
            pltpu.SemaphoreType.DMA((CHUNKS,)),
        ],
        compiler_params=pltpu.CompilerParams(collective_id=0, has_side_effects=True, vmem_limit_bytes=58 * 1024 * 1024),
    )(ci_vector, diagonal, alpha_coupling, beta_coupling, jnp.transpose(alpha_mask, (0, 2, 1, 3)), jnp.transpose(beta_mask, (0, 2, 1, 3)), alpha_partner, beta_partner, energy)


def solution(mesh):
    return jax.shard_map(
        local,
        mesh=mesh,
        in_specs=(
            P("alpha", "beta"),
            P("alpha", "beta"),
            P(),
            P("alpha", None),
            P("alpha", None, None, None),
            P("alpha", None, None, None),
            P("beta", None),
            P("beta", None, "alpha", None),
            P("beta", None, None, None),
        ),
        out_specs=P("alpha", "beta"),
        check_vma=False,
    )
```

```python
import jax
import jax.numpy as jnp
from jax import lax
from jax.experimental import pallas as pl
from jax.experimental.pallas import tpu as pltpu
from jax.sharding import PartitionSpec as P

MESH = pl.DeviceIdType.MESH
TILE = 896
BLOCK = 128
NBLK = TILE // BLOCK
CHUNKS = 7
ROWS = TILE // CHUNKS
PARTS = 7
PROWS = TILE // PARTS
START, EARLY = 5, 4
PIECE = 112
LEVELS = 32767.0
F32 = jnp.float32
BF16 = jnp.bfloat16
K0, X1, X2, Y1, Y2, Z2, Z3, Z4 = range(8)
ZR = 8


def chunk_rows(c):
    return pl.ds(ROWS * c, ROWS)


def flipped(index, bit):
    return index + (1 - 2 * ((index // bit) % 2)) * bit


def split(value):
    high = value.astype(BF16)
    return high, (value - high.astype(F32)).astype(BF16)


def pick(choices, rows, at):
    value = choices[0][at][rows, :]
    for choice in choices[1:]:
        value = lax.select(choice[0], choice[at][rows, :], value)
    return value.astype(F32)


def decode(choices, rows):
    scale = pick(choices, pl.ds(0, 8), 2)[0:1, 0:1]
    root = pick(choices, rows, 1) * (1.0 / LEVELS)
    return (root * jnp.abs(root)) * (root * root) * scale


def kernel(
    ci_hbm, diag_hbm, ac_hbm, bc_hbm, am, bm, ap, bp, energy, out_hbm,
    cv, dv, own, k0, x1, x2, y1, y2, z2, z3, z4, weights, piece, ha, hat, bl, xl, part, acc,
    head, h0, h1, h2, h3, h4, h5, h6, h7, load_sem, part_sem, send_sem, recv_sem, wsend_sem, wrecv_sem, hsend_sem, hrecv_sem, store_sem,
):
    tiles = [k0, x1, x2, y1, y2, z2, z3, z4]
    heads = [h0, h1, h2, h3, h4, h5, h6, h7]
    a = lax.axis_index("alpha")
    b = lax.axis_index("beta")
    y, xh = a % 4, a // 4
    core, xl_, z = b % 2, (b // 2) % 2, b // 4
    x = xh * 2 + xl_

    def at(dx=0, dy=0, dz=0, dc=0):
        nx, ny, nz = (x + dx + 4) % 4, (y + dy + 4) % 4, (z + dz + 8) % 8
        nc = (core + dc) % 2
        return ((nx // 2) * 4 + ny, nz * 4 + (nx % 2) * 2 + nc)

    tx = 1 - 2 * (x % 2)
    ty = 1 - 2 * (y % 2)
    tz = 1 - 2 * (z % 2)
    t = z % 4
    sz = 1 - 2 * (t // 2)
    inner = (t == 1) | (t == 2)

    def load_c(c):
        rows = pl.ds(c * PROWS, PROWS)
        return pltpu.make_async_copy(ci_hbm.at[rows, :], cv.at[rows, :], part_sem.at[c])

    load_p = pltpu.make_async_copy(bc_hbm.at[0], piece, load_sem.at[1])
    load_a = pltpu.make_async_copy(ac_hbm.at[0], ha, load_sem.at[2])
    load_d = pltpu.make_async_copy(diag_hbm, dv, load_sem.at[3])
    for c in range(PARTS):
        load_c(c).start()
    load_p.start()
    load_a.start()
    load_d.start()

    barrier = pltpu.get_barrier_semaphore()
    greet = [at(dc=1), at(dx=1), at(dx=-1), at(dx=2), at(dy=1), at(dy=-1), at(dy=2), at(dz=1), at(dz=-1), at(dz=2), at(dz=-2), at(dz=4)]
    for other in greet:
        pl.semaphore_signal(barrier, inc=1, device_id=other, device_id_type=MESH)

    def move(src, dst, lane, c, target):
        rows = chunk_rows(c)
        return pltpu.make_async_remote_copy(
            src_ref=src.at[rows, :],
            dst_ref=tiles[dst].at[rows, :],
            send_sem=send_sem.at[lane, c],
            recv_sem=recv_sem.at[dst, c],
            device_id=target,
            device_id_type=MESH,
        )

    def own_to_core(c):
        return move(own, K0, K0, c, at(dc=1))

    def own_to_x(c):
        return move(own, X1, X1, c, at(dx=tx))

    def pass_x(c):
        return move(x1, X2, X2, c, at(dx=-tx))

    def own_to_y(c):
        return move(own, Y1, Y1, c, at(dy=ty))

    def pass_y(c):
        return move(y1, Y2, Y2, c, at(dy=-ty))

    def own_to_z(c):
        return move(own, Z2, Z2, c, at(dz=tz))

    def own_to_z_far(c):
        return move(own, Z3, Z3, c, at(dz=2 * sz))

    def pass_z(c):
        return move(z2, Z3, ZR, c, at(dz=sz))

    def pass_z_far(c):
        return move(z3, Z4, Z4, c, at(dz=-2 * sz))

    def arrived(dst, c):
        rows = chunk_rows(c)
        pltpu.make_async_remote_copy(
            src_ref=tiles[dst].at[rows, :],
            dst_ref=tiles[dst].at[rows, :],
            send_sem=send_sem.at[dst, c],
            recv_sem=recv_sem.at[dst, c],
            device_id=at(dc=1),
            device_id_type=MESH,
        ).wait_recv()

    def wmove(ah, dy_src, lane, target):
        index = ((xh + ah) % 2) * 4 + (y + dy_src + 4) % 4
        rows = pl.ds(pl.multiple_of(index * PIECE, 16), PIECE)
        return pltpu.make_async_remote_copy(
            src_ref=weights.at[:, rows, :],
            dst_ref=weights.at[:, rows, :],
            send_sem=wsend_sem.at[lane],
            recv_sem=wrecv_sem.at[lane],
            device_id=target,
            device_id_type=MESH,
        )

    wsend = [
        wmove(0, 0, 0, at(dx=2)),
        wmove(0, 0, 1, at(dy=1)),
        wmove(0, 0, 2, at(dy=-1)),
        wmove(1, 0, 3, at(dy=1)),
        wmove(1, 0, 4, at(dy=-1)),
        wmove(0, -1, 5, at(dy=1)),
        wmove(1, 1, 6, at(dy=-1)),
    ]
    wrecv = [
        wmove(1, 0, 0, at(dx=2)),
        wmove(0, -1, 1, at(dy=1)),
        wmove(0, 1, 2, at(dy=1)),
        wmove(1, -1, 3, at(dy=1)),
        wmove(1, 1, 4, at(dy=1)),
        wmove(0, -2, 5, at(dy=1)),
        wmove(1, 2, 6, at(dy=1)),
    ]

    hsend = [
        pltpu.make_async_remote_copy(
            src_ref=head,
            dst_ref=heads[dst],
            send_sem=hsend_sem.at[dst],
            recv_sem=hrecv_sem.at[dst],
            device_id=target,
            device_id_type=MESH,
        )
        for dst, target in (
            (K0, at(dc=1)),
            (X1, at(dx=tx)),
            (X2, at(dx=2)),
            (Y1, at(dy=ty)),
            (Y2, at(dy=2)),
            (Z2, at(dz=tz)),
            (Z3, at(dz=2 - 4 * ((z // 2) % 2))),
            (Z4, at(dz=4)),
        )
    ]
    column = jnp.full((1, TILE), 1e-36, F32)
    for c in range(PARTS):
        load_c(c).wait()
        column = jnp.maximum(column, jnp.max(jnp.abs(cv[pl.ds(c * PROWS, PROWS), :]), axis=0, keepdims=True))
    top = jnp.max(column, axis=1, keepdims=True)
    exponent = jnp.maximum(jnp.floor(jnp.log2(top)) + 1.0, -120.0)
    head[...] = jnp.broadcast_to(jnp.exp2(exponent), (8, BLOCK))
    shrink = jnp.exp2(-exponent)

    def encode(c):
        value = cv[pl.ds(c * ROWS, ROWS), :]
        root = jnp.sqrt(jnp.sqrt(jnp.abs(value) * shrink)) * LEVELS
        root = jnp.minimum(jnp.round(root), LEVELS)
        own[chunk_rows(c), :] = jnp.where(value < 0, -root, root).astype(jnp.int16)

    def send_z(c):
        @pl.when(inner)
        def _():
            own_to_z_far(c).start()

        @pl.when(jnp.logical_not(inner))
        def _():
            own_to_z(c).start()

    encode(0)
    pl.semaphore_wait(barrier, len(greet))
    send_z(0)
    for c in range(1, CHUNKS):
        encode(c)
        send_z(c)

    load_p.wait()
    for s in range(2):
        for k in range(PIECE // 16):
            row = a * PIECE + 16 * k
            u = row // BLOCK
            rows = pl.ds(pl.multiple_of(row, 16), 16)
            for v in range(NBLK):
                columns = pl.ds(v * BLOCK, BLOCK)
                block = piece[s, pl.ds(16 * k, 16), columns].astype(F32)
                weights[s, rows, columns] = (block * bm[0, u, s, v].astype(F32)).astype(BF16)
    for lane in (0, 1, 2):
        wsend[lane].start()
    for copy in hsend:
        copy.start()
    for c in range(CHUNKS):
        own_to_x(c).start()
        own_to_y(c).start()
        own_to_core(c).start()

    load_a.wait()

    def mask_alpha(i):
        s, u = i // NBLK, i % NBLK
        for v in range(NBLK):
            block = ha[s, pl.ds(u * BLOCK, BLOCK), pl.ds(v * BLOCK, BLOCK)].astype(F32) * am[0, u, s, v].astype(F32)
            hat[pl.ds(v * BLOCK, BLOCK), pl.ds(s * TILE + u * BLOCK, BLOCK)] = block.T.astype(BF16)

    alpha_from = [[(ap[0, s] == flipped(a, bit), tiles[t], heads[t]) for bit, t in ((1, Y1), (2, Y2), (4, X2))] for s in range(2)]
    beta_from = [[(bp[0, s] == flipped(b, bit), tiles[t], heads[t]) for bit, t in ((1, K0), (2, X1), (4, Z2), (8, Z3), (16, Z4))] for s in range(2)]

    def alpha_operand():
        def body(c, _):
            rows = pl.ds(pl.multiple_of(c * PROWS, PROWS), PROWS)
            for s in range(2):
                high, low = split(decode(alpha_from[s], rows))
                to = pl.ds(pl.multiple_of(s * TILE + c * PROWS, PROWS), PROWS)
                for n in range(NBLK):
                    bl[n, to, pl.ds(0, BLOCK)] = high[:, n * BLOCK : (n + 1) * BLOCK]
                    bl[n, to, pl.ds(BLOCK, BLOCK)] = low[:, n * BLOCK : (n + 1) * BLOCK]
            return 0

        lax.fori_loop(0, PARTS, body, 0)

    def alpha_product(first, last):
        def body(i, _):
            n, m = i // 2, i % 2
            rows = pl.ds(pl.multiple_of(m * 448, 64), 448)
            both = jnp.dot(hat[rows, :], bl[n], preferred_element_type=F32)
            acc[rows, pl.ds(pl.multiple_of(n * BLOCK, BLOCK), BLOCK)] += both[:, :BLOCK] + both[:, BLOCK:]
            return 0

        lax.fori_loop(2 * first, 2 * last, body, 0)

    def beta_product(first, count):
        rows = pl.ds(first, count)
        for s in range(2):
            high, low = split(decode(beta_from[s], rows))
            xl[s, pl.ds(0, count), :] = high
            xl[s, pl.ds(count, count), :] = low

        both = pl.ds(0, 2 * count)
        for s in range(2):
            for k in (pl.ds(0, 512), pl.ds(512, TILE - 512)):
                product = jnp.dot(xl[s, both, k], weights[s, k, :], preferred_element_type=F32)
                if s == 0 and k.start == 0:
                    part[both, :] = product
                else:
                    part[both, :] += product
        acc[rows, :] += part[pl.ds(0, count), :] + part[pl.ds(count, count), :]

    def correct(first, count):
        rows = pl.ds(first, count)
        gap = dv[rows, :] - energy[0]
        acc[rows, :] = (acc[rows, :] - energy[0] * cv[rows, :]) * gap / (gap * gap + 0.0625)

    def complete(c):
        arrived(K0, c)

        @pl.when(jnp.logical_not(inner))
        def _():
            arrived(Z2, c)

        arrived(Z4, c)

    def store(c):
        rows = chunk_rows(c)
        return pltpu.make_async_copy(acc.at[rows, :], out_hbm.at[rows, :], store_sem.at[c])

    acc[...] = jnp.zeros_like(acc)
    far, side = 2, 2
    for step in range(CHUNKS + side):
        c = step
        if c < CHUNKS:

            @pl.when(inner)
            def _():
                arrived(Z2, c)
                pass_z(c).start()

        c = step - far
        if 0 <= c < CHUNKS:
            arrived(Z3, c)
            pass_z_far(c).start()

            @pl.when(inner)
            def _():
                own_to_z(c).start()

        c = step - side
        if 0 <= c < CHUNKS:
            arrived(X1, c)
            pass_x(c).start()
            arrived(Y1, c)
            pass_y(c).start()
        if step < NBLK:
            mask_alpha(2 * step)
            mask_alpha(2 * step + 1)
        if step == 1:
            wrecv[0].wait_recv()
            wsend[3].start()
            wsend[4].start()
        if step == 2:
            wrecv[1].wait_recv()
            wsend[5].start()
        if step == 3:
            wrecv[4].wait_recv()
            wsend[6].start()
        if step == START:
            for dst in range(8):
                hsend[dst].wait_recv()
            for lane in (2, 3, 5, 6):
                wrecv[lane].wait_recv()
        if step >= START and step - START < EARLY:
            p = step - START
            complete(p)
            beta_product(p * PROWS, PROWS)

    for c in range(CHUNKS):
        arrived(X2, c)
        arrived(Y2, c)
    alpha_operand()
    alpha_product(0, NBLK)
    load_d.wait()
    for p in range(EARLY):
        correct(p * PROWS, PROWS)
        store(p).start()
    for group in [(c,) for c in range(EARLY, CHUNKS)]:
        for c in group:
            complete(c)
        beta_product(group[0] * ROWS, len(group) * ROWS)
        correct(group[0] * ROWS, len(group) * ROWS)
        for c in group:
            store(c).start()

    for copy in hsend:
        copy.wait_send()
    for c in range(CHUNKS):
        store(c).wait()
    for c in range(CHUNKS):
        for copy in (own_to_core(c), own_to_x(c), pass_x(c), own_to_y(c), pass_y(c), own_to_z(c), pass_z_far(c)):
            copy.wait_send()

        @pl.when(inner)
        def _():
            own_to_z_far(c).wait_send()
            pass_z(c).wait_send()

    for copy in wsend:
        copy.wait_send()


def local(ci_vector, diagonal, energy, alpha_partner, alpha_coupling, alpha_mask, beta_partner, beta_coupling, beta_mask):
    anywhere = pl.BlockSpec(memory_space=pltpu.HBM)
    scalars = pl.BlockSpec(memory_space=pltpu.SMEM)
    code = pltpu.VMEM((TILE, TILE), jnp.int16)
    return pl.pallas_call(
        kernel,
        out_shape=jax.ShapeDtypeStruct((TILE, TILE), F32),
        in_specs=[anywhere] * 4 + [scalars] * 5,
        out_specs=anywhere,
        scratch_shapes=[pltpu.VMEM((TILE, TILE), F32)] * 2
        + [code] * 9
        + [
            pltpu.VMEM((2, TILE, TILE), BF16),
            pltpu.VMEM((2, PIECE, TILE), BF16),
            pltpu.VMEM((2, TILE, TILE), BF16),
            pltpu.VMEM((TILE, 2 * TILE), BF16),
            pltpu.VMEM((NBLK, 2 * TILE, 2 * BLOCK), BF16),
            pltpu.VMEM((2, 2 * PROWS, TILE), BF16),
            pltpu.VMEM((2 * PROWS, TILE), F32),
            pltpu.VMEM((TILE, TILE), F32),
        ]
        + [pltpu.VMEM((8, BLOCK), F32)] * 9
        + [
            pltpu.SemaphoreType.DMA((4,)),
            pltpu.SemaphoreType.DMA((PARTS,)),
            pltpu.SemaphoreType.DMA((9, CHUNKS)),
            pltpu.SemaphoreType.DMA((8, CHUNKS)),
            pltpu.SemaphoreType.DMA((7,)),
            pltpu.SemaphoreType.DMA((7,)),
            pltpu.SemaphoreType.DMA((8,)),
            pltpu.SemaphoreType.DMA((8,)),
            pltpu.SemaphoreType.DMA((CHUNKS,)),
        ],
        compiler_params=pltpu.CompilerParams(collective_id=0, has_side_effects=True, vmem_limit_bytes=58 * 1024 * 1024),
    )(ci_vector, diagonal, alpha_coupling, beta_coupling, jnp.transpose(alpha_mask, (0, 2, 1, 3)), jnp.transpose(beta_mask, (0, 2, 1, 3)), alpha_partner, beta_partner, energy)


def solution(mesh):
    return jax.shard_map(
        local,
        mesh=mesh,
        in_specs=(
            P("alpha", "beta"),
            P("alpha", "beta"),
            P(),
            P("alpha", None),
            P("alpha", None, None, None),
            P("alpha", None, None, None),
            P("beta", None),
            P("beta", None, "alpha", None),
            P("beta", None, None, None),
        ),
        out_specs=P("alpha", "beta"),
        check_vma=False,
    )
```
